512 devices in a mesh: group: 4 (over y), shard: 32 (over x_hi, z), tensor: 4 (over x_lo, core).
Axes of the slice: x: 4 (x_hi: 2, x_lo: 2; x = x_hi * 2 + x_lo), y: 4, z: 16, core: 2. Of those that a mesh axis runs over, the one named last changes fastest.
Arguments:
- mlp_deltas: bfloat16 [4, 3, 2560, 6400], P('group', None, 'shard', 'tensor'), may hold values from -6 to 6
- mlp_master: float32 [3, 2560, 6400], P(None, ('group', 'shard', 'tensor')), may hold values from -6 to 6
- mlp_momentum: float32 [3, 2560, 6400], P(None, ('group', 'shard', 'tensor')), may hold values from -3 to 3
- attn_deltas: bfloat16 [4, 2560, 2560], P('group', 'shard', 'tensor'), may hold values from -6 to 6
- attn_master: float32 [2560, 2560], P(('group', 'shard', 'tensor')), may hold values from -6 to 6
- attn_momentum: float32 [2560, 2560], P(('group', 'shard', 'tensor')), may hold values from -3 to 3
Outputs:
- new_mlp_master: float32 [3, 2560, 6400], P(None, ('group', 'shard', 'tensor'))
- new_mlp_momentum: float32 [3, 2560, 6400], P(None, ('group', 'shard', 'tensor'))
- mlp_weights: bfloat16 [3, 2560, 6400], P(None, 'shard', 'tensor')
- new_attn_master: float32 [2560, 2560], P(('group', 'shard', 'tensor'))
- new_attn_momentum: float32 [2560, 2560], P(('group', 'shard', 'tensor'))
- attn_weights: bfloat16 [2560, 2560], P('shard', 'tensor')
The draws below stay inside these ranges and needn't reach their ends.
All inputs are finite; a program needn't handle non-finite values.
Results may differ from the reference program's by a relative error of at most 0.0075.
Values may be sent and summed in bfloat16 or wider, within the bound.
A program may use at most 64 MiB of HBM per device.

```python
import jax
import jax.numpy as jnp

D = 2560
FF = 6400
HV = 2560
GROUPS = 4
N_GROUP = 4


def shard_levels(rng, shape, cuts, smallest, high):
    level = 1.0
    for dim, shards_of in cuts:
        steps = jax.random.uniform(jax.random.fold_in(jax.random.fold_in(rng, 6), dim), (shards_of,), jnp.float32, smallest / len(cuts), high / len(cuts))
        level = level * jnp.repeat(jnp.exp(steps), shape[dim] // shards_of).reshape((-1,) + (1,) * (len(shape) - 1 - dim))
    return level


def centred(own_key, extent, scale, most, split=(), kind=jnp.bfloat16):
    values = scale * jax.random.normal(own_key, extent, jnp.float32)
    if split:
        values = values * shard_levels(own_key, extent, split, -0.22, 0.18)
    return jnp.clip(values, -most, most).astype(kind)


def setup_inputs(seed: int = 0) -> dict:
    arg_keys = jax.random.split(jax.random.key(seed), 7)
    return {
        "mlp_deltas": centred(arg_keys[0], (GROUPS, 3, D, FF), 1.0, 6.0, ((0, 4), (2, 32), (3, 4))),
        "mlp_master": centred(arg_keys[1], (3, D, FF), 1.0, 6.0, ((1, 512),), jnp.float32),
        "mlp_momentum": centred(arg_keys[2], (3, D, FF), 0.5, 3.0, ((1, 512),), jnp.float32),
        "attn_deltas": centred(arg_keys[3], (GROUPS, D, HV), 1.0, 6.0, ((0, 4), (1, 32), (2, 4))),
        "attn_master": centred(arg_keys[4], (D, HV), 1.0, 6.0, ((0, 512),), jnp.float32),
        "attn_momentum": centred(arg_keys[5], (D, HV), 0.5, 3.0, ((0, 512),), jnp.float32),
    }


momentum_decay = 0.9
outer_rate = 0.7


def outer_step(deltas, master, momentum):
    total = jnp.zeros(deltas.shape[1:], jnp.float32)
    for member in range(N_GROUP):
        total = total + deltas[member].astype(jnp.float32)
    outer_grad = total / N_GROUP
    new_momentum = momentum_decay * momentum + outer_grad
    new_master = master - outer_rate * (outer_grad + momentum_decay * new_momentum)
    weights = new_master.astype(jnp.bfloat16)
    return new_master, new_momentum, weights


def reference(mlp_deltas, mlp_master, mlp_momentum, attn_deltas, attn_master, attn_momentum):
    mlp_new, mlp_moment, mlp_weights = outer_step(mlp_deltas, mlp_master, mlp_momentum)
    attn_new, attn_moment, attn_weights = outer_step(attn_deltas, attn_master, attn_momentum)
    return mlp_new, mlp_moment, mlp_weights, attn_new, attn_moment, attn_weights
```

```python
import functools

import jax
import jax.numpy as jnp
from jax import lax
from jax.experimental import pallas as pl
from jax.experimental.pallas import tpu as pltpu
from jax.sharding import PartitionSpec as P

momentum_decay = 0.9
outer_rate = 0.7

LANES = 128
UNIT = 5
GROUPS = 4
TENSORS = 4
OWNERS = 16
MLP_TILES = 13
ATTN_TILES = 5
TILES = 3 * MLP_TILES + ATTN_TILES
PART = TILES // GROUPS
CHUNKS = ((0, 11),)
MESH = pl.DeviceIdType.MESH


def chunk_rows(count):
    return -(-UNIT * count // 8) * 8


def tile_place(tile):
    if tile < 3 * MLP_TILES:
        return tile // MLP_TILES, tile % MLP_TILES
    return 3, tile - 3 * MLP_TILES


def tile_width(tile):
    matrix, column = tile_place(tile)
    return 64 if matrix < 3 and column == MLP_TILES - 1 else LANES


def remote(src, dst, send_sem, recv_sem, device):
    return pltpu.make_async_remote_copy(
        src_ref=src, dst_ref=dst, send_sem=send_sem, recv_sem=recv_sem,
        device_id=device, device_id_type=MESH,
    )


def kernel(
    x_ref, master_ref, mom_ref, ax_ref, amaster_ref, amom_ref,
    new_master, new_mom, weights, new_amaster, new_amom, aweights,
    tiles, sums, total, out_tiles, *rest,
):
    count = len(CHUNKS)
    per_chunk, sems = rest[: 6 * count], rest[6 * count:]
    stage = per_chunk[0::6]
    sum_send = per_chunk[1::6]
    sum_recv = per_chunk[2::6]
    held_master = per_chunk[3::6]
    held_mom = per_chunk[4::6]
    weight_recv = per_chunk[5::6]
    (a_send, a_recv, b_send, b_recv, d_send, d_recv, e_send, e_recv, local_sem) = sems

    g = lax.axis_index("group")
    s = lax.axis_index("shard")
    t = lax.axis_index("tensor")
    my_owner = lax.rem(s, 4) * 4 + t

    def peer(step):
        return (lax.rem(g + step, GROUPS), s, t)

    def owner(k):
        return (s // 8, 4 * lax.rem(s, 8) + k // 4, lax.rem(k, 4))

    def trainer(p):
        return (p // 4, g * 8 + s // 4, lax.rem(p, 4))

    def is_me(device):
        return (device[0] == g) & (device[1] == s) & (device[2] == t)

    barrier = pltpu.get_barrier_semaphore()
    for step in range(1, GROUPS):
        pl.semaphore_signal(barrier, inc=1, device_id=peer(step), device_id_type=MESH)

    def greet(k, carry):
        for device in (owner(k), trainer(k)):
            mine = is_me(device)

            @pl.when(jnp.logical_not(mine))
            def _():
                pl.semaphore_signal(barrier, inc=1, device_id=device, device_id_type=MESH)

        return carry

    lax.fori_loop(0, OWNERS, greet, 0)

    for tile in range(TILES):
        matrix, column = tile_place(tile)
        width = tile_width(tile)
        columns = slice(LANES * column, LANES * column + width)
        block = x_ref[matrix, :, columns] if matrix < 3 else ax_ref[:, columns]
        tiles[tile, :, 0:width] = block

    own_trainer = is_me(owner(my_owner)).astype(jnp.int32)
    pl.semaphore_wait(barrier, GROUPS - 1 + 2 * (OWNERS - own_trainer))

    def a_copy(c, step):
        q0, n = CHUNKS[c]
        to = lax.rem(g + step, GROUPS)
        return remote(
            tiles.at[pl.ds(PART * to + q0, n)], sums.at[g, pl.ds(q0, n)],
            a_send.at[c, step], a_recv.at[c, g], peer(step),
        )

    def a_arrival(c, step):
        q0, n = CHUNKS[c]
        source = lax.rem(g + step, GROUPS)
        return remote(
            sums.at[source, pl.ds(q0, n)], sums.at[source, pl.ds(q0, n)],
            a_send.at[c, step], a_recv.at[c, source], peer(step),
        )

    for c in range(count):
        for step in (2, 1, 3):
            a_copy(c, step).start()

    for c, (q0, n) in enumerate(CHUNKS):
        for part in range(GROUPS):
            for q in range(n):
                tile = PART * part + q0 + q
                matrix, column = tile_place(tile)
                width = tile_width(tile)
                for piece in range(TENSORS):
                    slot = part * TENSORS + piece
                    rows = slice(UNIT * q, UNIT * q + UNIT)
                    for held, mlp, attn in (
                        (held_master[c], master_ref, amaster_ref), (held_mom[c], mom_ref, amom_ref),
                    ):
                        if matrix < 3:
                            start = 1600 * piece + LANES * column
                            held[slot, rows, 0:width] = mlp[matrix, :, start:start + width]
                        else:
                            start = 640 * piece + LANES * column
                            held[slot, rows, :] = attn[:, start:start + width]

    def b_copy(c, k):
        return remote(
            sum_send[c].at[k], sum_recv[c].at[g * TENSORS + t],
            b_send.at[c, k], b_recv.at[c, g * TENSORS + t], owner(k),
        )

    def d_copy(c, p):
        return remote(
            sum_recv[c].at[p], weight_recv[c].at[my_owner],
            d_send.at[c, p], d_recv.at[c, my_owner], trainer(p),
        )

    for c, (q0, n) in enumerate(CHUNKS):
        for step in range(1, GROUPS):
            a_arrival(c, step).wait_recv()
        sources = [lax.rem(g + step, GROUPS) for step in range(1, GROUPS)]
        for q in range(q0, q0 + n):
            value = tiles[PART * g + q].astype(jnp.float32)
            for source in sources:
                value = value + sums[source, q].astype(jnp.float32)
            total[q] = value
        for k in range(OWNERS):
            for q in range(n):
                stage[c][k, UNIT * q:UNIT * q + UNIT, :] = total[q0 + q, UNIT * k:UNIT * k + UNIT, :]

        def hand_out(k, carry):
            sum_send[c][k] = stage[c][k].astype(jnp.bfloat16)
            mine = is_me(owner(k))

            @pl.when(jnp.logical_not(mine))
            def _():
                b_copy(c, k).start()

            @pl.when(mine)
            def _():
                here = pltpu.make_async_copy(
                    sum_send[c].at[k], sum_recv[c].at[g * TENSORS + t], local_sem
                )
                here.start()
                here.wait()

            return carry

        lax.fori_loop(0, OWNERS, hand_out, 0)

    for c in range(count):

        def step_rows(p, carry):
            mine = is_me(trainer(p))

            @pl.when(jnp.logical_not(mine))
            def _():
                remote(
                    sum_recv[c].at[p], sum_recv[c].at[p], b_send.at[c, p], b_recv.at[c, p], trainer(p)
                ).wait_recv()

            grad = sum_recv[c][p].astype(jnp.float32) / GROUPS
            momentum = momentum_decay * held_mom[c][p] + grad
            master = held_master[c][p] - outer_rate * (grad + momentum_decay * momentum)
            held_mom[c][p] = momentum
            held_master[c][p] = master
            sum_recv[c][p] = master.astype(jnp.bfloat16)

            @pl.when(jnp.logical_not(mine))
            def _():
                d_copy(c, p).start()

            @pl.when(mine)
            def _():
                here = pltpu.make_async_copy(
                    sum_recv[c].at[p], weight_recv[c].at[my_owner], local_sem
                )
                here.start()
                here.wait()

            return carry

        lax.fori_loop(0, OWNERS, step_rows, 0)

    for c, (q0, n) in enumerate(CHUNKS):
        for part in range(GROUPS):
            for q in range(n):
                tile = PART * part + q0 + q
                matrix, column = tile_place(tile)
                width = tile_width(tile)
                for piece in range(TENSORS):
                    slot = part * TENSORS + piece
                    rows = slice(UNIT * q, UNIT * q + UNIT)
                    for held, mlp, attn in (
                        (held_master[c], new_master, new_amaster), (held_mom[c], new_mom, new_amom),
                    ):
                        if matrix < 3:
                            start = 1600 * piece + LANES * column
                            mlp[matrix, :, start:start + width] = held[slot, rows, 0:width]
                        else:
                            start = 640 * piece + LANES * column
                            attn[:, start:start + width] = held[slot, rows, :]

    def e_copy(c, step):
        q0, n = CHUNKS[c]
        part = out_tiles.at[pl.ds(PART * g + q0, n)]
        return remote(part, part, e_send.at[c, step], e_recv.at[c, g], peer(step))

    def e_arrival(c, step):
        q0, n = CHUNKS[c]
        source = lax.rem(g + step, GROUPS)
        part = out_tiles.at[pl.ds(PART * source + q0, n)]
        return remote(part, part, e_send.at[c, step], e_recv.at[c, source], peer(step))

    for c, (q0, n) in enumerate(CHUNKS):

        def take_in(k, carry):
            @pl.when(jnp.logical_not(is_me(owner(k))))
            def _():
                remote(
                    weight_recv[c].at[k], weight_recv[c].at[k], d_send.at[c, k], d_recv.at[c, k], owner(k)
                ).wait_recv()

            stage[c][k] = weight_recv[c][k].astype(jnp.float32)
            return carry

        lax.fori_loop(0, OWNERS, take_in, 0)
        for k in range(OWNERS):
            for q in range(n):
                total[q0 + q, UNIT * k:UNIT * k + UNIT, :] = stage[c][k, UNIT * q:UNIT * q + UNIT, :]
        for q in range(q0, q0 + n):
            out_tiles[PART * g + q] = total[q].astype(jnp.bfloat16)
        for step in (2, 1, 3):
            e_copy(c, step).start()

    for c in range(count):
        for step in range(1, GROUPS):
            e_arrival(c, step).wait_recv()
    for tile in range(TILES):
        matrix, column = tile_place(tile)
        width = tile_width(tile)
        columns = slice(LANES * column, LANES * column + width)
        if matrix < 3:
            weights[matrix, :, columns] = out_tiles[tile, :, 0:width]
        else:
            aweights[:, columns] = out_tiles[tile]

    for c in range(count):
        for step in range(1, GROUPS):
            a_copy(c, step).wait_send()
            e_copy(c, step).wait_send()

        def drain(k, carry):
            @pl.when(jnp.logical_not(is_me(owner(k))))
            def _():
                b_copy(c, k).wait_send()

            @pl.when(jnp.logical_not(is_me(trainer(k))))
            def _():
                d_copy(c, k).wait_send()

            return carry

        lax.fori_loop(0, OWNERS, drain, 0)


def local(mlp_deltas, mlp_master, mlp_momentum, attn_deltas, attn_master, attn_momentum):
    x, ax = mlp_deltas[0], attn_deltas[0]
    rows = x.shape[1]
    f32, bf16 = jnp.float32, jnp.bfloat16
    scratch = [
        pltpu.VMEM((TILES, rows, LANES), bf16),
        pltpu.VMEM((GROUPS, PART, rows, LANES), bf16),
        pltpu.VMEM((PART, rows, LANES), f32),
        pltpu.VMEM((TILES, rows, LANES), bf16),
    ]
    for _, n in CHUNKS:
        shape = (OWNERS, chunk_rows(n), LANES)
        for kind in (f32, bf16, bf16, f32, f32, bf16):
            scratch.append(pltpu.VMEM(shape, kind))
    count = len(CHUNKS)
    DMA = pltpu.SemaphoreType.DMA
    scratch += [
        DMA((count, GROUPS)), DMA((count, GROUPS)),
        DMA((count, OWNERS)), DMA((count, OWNERS)),
        DMA((count, OWNERS)), DMA((count, OWNERS)),
        DMA((count, GROUPS)), DMA((count, GROUPS)),
        DMA(()),
    ]
    shapes = [
        jax.ShapeDtypeStruct(mlp_master.shape, f32),
        jax.ShapeDtypeStruct(mlp_momentum.shape, f32),
        jax.ShapeDtypeStruct(x.shape, bf16),
        jax.ShapeDtypeStruct(attn_master.shape, f32),
        jax.ShapeDtypeStruct(attn_momentum.shape, f32),
        jax.ShapeDtypeStruct(ax.shape, bf16),
    ]
    vmem = pl.BlockSpec(memory_space=pltpu.VMEM)
    return pl.pallas_call(
        kernel,
        out_shape=shapes,
        in_specs=[vmem] * 6,
        out_specs=[vmem] * 6,
        scratch_shapes=scratch,
        compiler_params=pltpu.CompilerParams(collective_id=0, has_side_effects=True),
    )(x, mlp_master, mlp_momentum, ax, attn_master, attn_momentum)


def solution(mesh):
    owned = P(None, ("group", "shard", "tensor"), None)
    attn_owned = P(("group", "shard", "tensor"), None)
    return jax.shard_map(
        local,
        mesh=mesh,
        in_specs=(
            P("group", None, "shard", "tensor"), owned, owned,
            P("group", "shard", "tensor"), attn_owned, attn_owned,
        ),
        out_specs=(
            owned, owned, P(None, "shard", "tensor"),
            attn_owned, attn_owned, P("shard", "tensor"),
        ),
        check_vma=False,
    )
```

```python
import functools

import jax
import jax.numpy as jnp
from jax import lax
from jax.experimental import pallas as pl
from jax.experimental.pallas import tpu as pltpu
from jax.sharding import PartitionSpec as P

momentum_decay = 0.9
outer_rate = 0.7

LANES = 128
UNIT = 5
GROUPS = 4
TENSORS = 4
OWNERS = 16
MLP_TILES = 13
ATTN_TILES = 5
TILES = 3 * MLP_TILES + ATTN_TILES
PART = TILES // GROUPS
CHUNKS = ((0, 3), (3, 8))
MESH = pl.DeviceIdType.MESH


def chunk_rows(count):
    return -(-UNIT * count // 8) * 8


def tile_place(tile):
    if tile < 3 * MLP_TILES:
        return tile // MLP_TILES, tile % MLP_TILES
    return 3, tile - 3 * MLP_TILES


def tile_width(tile):
    matrix, column = tile_place(tile)
    return 64 if matrix < 3 and column == MLP_TILES - 1 else LANES


def remote(src, dst, send_sem, recv_sem, device):
    return pltpu.make_async_remote_copy(
        src_ref=src, dst_ref=dst, send_sem=send_sem, recv_sem=recv_sem,
        device_id=device, device_id_type=MESH,
    )


def kernel(
    x_ref, master_ref, mom_ref, ax_ref, amaster_ref, amom_ref,
    new_master, new_mom, weights, new_amaster, new_amom, aweights,
    tiles, sums, total, out_tiles, *rest,
):
    count = len(CHUNKS)
    per_chunk, sems = rest[: 7 * count], rest[7 * count:]
    stage = per_chunk[0::7]
    sum_send = per_chunk[1::7]
    sum_recv = per_chunk[2::7]
    held_master = per_chunk[3::7]
    held_mom = per_chunk[4::7]
    weight_recv = per_chunk[5::7]
    relay = per_chunk[6::7]
    (a_send, a_recv, b_send, b_recv, d_send, d_recv, r_send, r_recv, e_send, e_recv, local_sem) = sems

    g = lax.axis_index("group")
    s = lax.axis_index("shard")
    t = lax.axis_index("tensor")
    my_owner = lax.rem(s, 4) * 4 + t

    def peer(step):
        return (lax.rem(g + step, GROUPS), s, t)

    def owner(k):
        return (s // 8, 4 * lax.rem(s, 8) + k // 4, lax.rem(k, 4))

    def trainer(p):
        return (p // 4, g * 8 + s // 4, lax.rem(p, 4))

    x_hi, z = s // 16, lax.rem(s, 16)

    def hub(p):
        return (p // 4, 16 * (g // 2) + z, lax.rem(p, 4))

    def hub_source(slot):
        return (2 * x_hi + slot // 8, 16 * lax.rem(slot // 4, 2) + z, lax.rem(slot, 4))

    def relay_to(w):
        return (g, 16 * x_hi + 4 * w + z // 4, t)

    def relay_source(j):
        return (g, 16 * x_hi + 4 * lax.rem(z, 4) + j, t)

    def is_me(device):
        return (device[0] == g) & (device[1] == s) & (device[2] == t)

    def unless_me(device, action):
        pl.when(jnp.logical_not(is_me(device)))(action)

    barrier = pltpu.get_barrier_semaphore()

    def greet(device):
        pl.semaphore_signal(barrier, inc=1, device_id=device, device_id_type=MESH)

    def greet_senders(k, carry):
        unless_me(trainer(k), lambda: greet(trainer(k)))
        unless_me(hub_source(k), lambda: greet(hub_source(k)))
        return carry

    def greet_relays(j, carry):
        unless_me(relay_source(j), lambda: greet(relay_source(j)))
        return carry

    for step in range(1, GROUPS):
        greet(peer(step))
    lax.fori_loop(0, OWNERS, greet_senders, 0)
    lax.fori_loop(0, 4, greet_relays, 0)
    own_slot = 4 * (2 * lax.rem(g, 2) + x_hi) + t
    waits = (
        GROUPS - 1 + 2 * OWNERS + 4
        - is_me(owner(my_owner)).astype(jnp.int32)
        - is_me(hub(GROUPS * g + t)).astype(jnp.int32)
        - is_me(relay_to(z // 4)).astype(jnp.int32)
    )

    for tile in range(TILES):
        matrix, column = tile_place(tile)
        width = tile_width(tile)
        columns = slice(LANES * column, LANES * column + width)
        block = x_ref[matrix, :, columns] if matrix < 3 else ax_ref[:, columns]
        tiles[tile, :, 0:width] = block

    pl.semaphore_wait(barrier, waits)

    def a_copy(c, step):
        q0, n = CHUNKS[c]
        to = lax.rem(g + step, GROUPS)
        return remote(
            tiles.at[pl.ds(PART * to + q0, n)], sums.at[g, pl.ds(q0, n)],
            a_send.at[c, step], a_recv.at[c, g], peer(step),
        )

    def a_arrival(c, step):
        q0, n = CHUNKS[c]
        source = lax.rem(g + step, GROUPS)
        return remote(
            sums.at[source, pl.ds(q0, n)], sums.at[source, pl.ds(q0, n)],
            a_send.at[c, step], a_recv.at[c, source], peer(step),
        )

    for c in range(count):
        for step in (2, 1, 3):
            a_copy(c, step).start()

    for c, (q0, n) in enumerate(CHUNKS):
        for part in range(GROUPS):
            for q in range(n):
                tile = PART * part + q0 + q
                matrix, column = tile_place(tile)
                width = tile_width(tile)
                for piece in range(TENSORS):
                    slot = part * TENSORS + piece
                    rows = slice(UNIT * q, UNIT * q + UNIT)
                    for held, mlp, attn in (
                        (held_master[c], master_ref, amaster_ref), (held_mom[c], mom_ref, amom_ref),
                    ):
                        if matrix < 3:
                            start = 1600 * piece + LANES * column
                            held[slot, rows, 0:width] = mlp[matrix, :, start:start + width]
                        else:
                            start = 640 * piece + LANES * column
                            held[slot, rows, :] = attn[:, start:start + width]

    def b_copy(c, k):
        return remote(
            sum_send[c].at[k], sum_recv[c].at[g * TENSORS + t],
            b_send.at[c, k], b_recv.at[c, g * TENSORS + t], owner(k),
        )

    def d_copy(c, p):
        return remote(
            sum_recv[c].at[p], relay[c].at[own_slot],
            d_send.at[c, p], d_recv.at[c, own_slot], hub(p),
        )

    def r_copy(c, w):
        bundle = pl.ds(4 * lax.rem(z, 4), 4)
        return remote(
            relay[c].at[pl.ds(4 * w, 4)], weight_recv[c].at[bundle],
            r_send.at[c, w], r_recv.at[c, lax.rem(z, 4)], relay_to(w),
        )

    for c, (q0, n) in enumerate(CHUNKS):
        for step in range(1, GROUPS):
            a_arrival(c, step).wait_recv()
        sources = [lax.rem(g + step, GROUPS) for step in range(1, GROUPS)]
        for q in range(q0, q0 + n):
            value = tiles[PART * g + q].astype(jnp.float32)
            for source in sources:
                value = value + sums[source, q].astype(jnp.float32)
            total[q] = value
        for k in range(OWNERS):
            for q in range(n):
                stage[c][k, UNIT * q:UNIT * q + UNIT, :] = total[q0 + q, UNIT * k:UNIT * k + UNIT, :]

        def hand_out(k, carry):
            sum_send[c][k] = stage[c][k].astype(jnp.bfloat16)
            mine = is_me(owner(k))

            @pl.when(jnp.logical_not(mine))
            def _():
                b_copy(c, k).start()

            @pl.when(mine)
            def _():
                here = pltpu.make_async_copy(
                    sum_send[c].at[k], sum_recv[c].at[g * TENSORS + t], local_sem
                )
                here.start()
                here.wait()

            return carry

        lax.fori_loop(0, OWNERS, hand_out, 0)

    for c in range(count):

        def step_rows(p, carry):
            mine = is_me(trainer(p))

            @pl.when(jnp.logical_not(mine))
            def _():
                remote(
                    sum_recv[c].at[p], sum_recv[c].at[p], b_send.at[c, p], b_recv.at[c, p], trainer(p)
                ).wait_recv()

            grad = sum_recv[c][p].astype(jnp.float32) / GROUPS
            momentum = momentum_decay * held_mom[c][p] + grad
            master = held_master[c][p] - outer_rate * (grad + momentum_decay * momentum)
            held_mom[c][p] = momentum
            held_master[c][p] = master
            sum_recv[c][p] = master.astype(jnp.bfloat16)

            to_me = is_me(hub(p))

            @pl.when(jnp.logical_not(to_me))
            def _():
                d_copy(c, p).start()

            @pl.when(to_me)
            def _():
                here = pltpu.make_async_copy(
                    sum_recv[c].at[p], relay[c].at[own_slot], local_sem
                )
                here.start()
                here.wait()

            return carry

        lax.fori_loop(0, OWNERS, step_rows, 0)

    for c in range(count):

        def pass_on(w, carry):
            for piece in range(TENSORS):
                slot = 4 * w + piece

                @pl.when(jnp.logical_not(is_me(hub_source(slot))))
                def _():
                    remote(
                        relay[c].at[slot], relay[c].at[slot],
                        d_send.at[c, slot], d_recv.at[c, slot], hub_source(slot),
                    ).wait_recv()

            mine = is_me(relay_to(w))

            @pl.when(jnp.logical_not(mine))
            def _():
                r_copy(c, w).start()

            @pl.when(mine)
            def _():
                here = pltpu.make_async_copy(
                    relay[c].at[pl.ds(4 * w, 4)],
                    weight_recv[c].at[pl.ds(4 * lax.rem(z, 4), 4)], local_sem,
                )
                here.start()
                here.wait()

            return carry

        lax.fori_loop(0, 4, pass_on, 0)

    for c, (q0, n) in enumerate(CHUNKS):
        for part in range(GROUPS):
            for q in range(n):
                tile = PART * part + q0 + q
                matrix, column = tile_place(tile)
                width = tile_width(tile)
                for piece in range(TENSORS):
                    slot = part * TENSORS + piece
                    rows = slice(UNIT * q, UNIT * q + UNIT)
                    for held, mlp, attn in (
                        (held_master[c], new_master, new_amaster), (held_mom[c], new_mom, new_amom),
                    ):
                        if matrix < 3:
                            start = 1600 * piece + LANES * column
                            mlp[matrix, :, start:start + width] = held[slot, rows, 0:width]
                        else:
                            start = 640 * piece + LANES * column
                            attn[:, start:start + width] = held[slot, rows, :]

    def e_copy(c, step):
        q0, n = CHUNKS[c]
        part = out_tiles.at[pl.ds(PART * g + q0, n)]
        return remote(part, part, e_send.at[c, step], e_recv.at[c, g], peer(step))

    def e_arrival(c, step):
        q0, n = CHUNKS[c]
        source = lax.rem(g + step, GROUPS)
        part = out_tiles.at[pl.ds(PART * source + q0, n)]
        return remote(part, part, e_send.at[c, step], e_recv.at[c, source], peer(step))

    for c, (q0, n) in enumerate(CHUNKS):

        def take_in(j, carry):
            bundle = weight_recv[c].at[pl.ds(4 * j, 4)]

            @pl.when(jnp.logical_not(is_me(relay_source(j))))
            def _():
                remote(
                    bundle, bundle, r_send.at[c, j], r_recv.at[c, j], relay_source(j)
                ).wait_recv()

            for piece in range(TENSORS):
                stage[c][4 * j + piece] = weight_recv[c][4 * j + piece].astype(jnp.float32)
            return carry

        lax.fori_loop(0, 4, take_in, 0)
        for k in range(OWNERS):
            for q in range(n):
                total[q0 + q, UNIT * k:UNIT * k + UNIT, :] = stage[c][k, UNIT * q:UNIT * q + UNIT, :]
        for q in range(q0, q0 + n):
            out_tiles[PART * g + q] = total[q].astype(jnp.bfloat16)
        for step in (2, 1, 3):
            e_copy(c, step).start()

    for c in range(count):
        for step in range(1, GROUPS):
            e_arrival(c, step).wait_recv()
    for tile in range(TILES):
        matrix, column = tile_place(tile)
        width = tile_width(tile)
        columns = slice(LANES * column, LANES * column + width)
        if matrix < 3:
            weights[matrix, :, columns] = out_tiles[tile, :, 0:width]
        else:
            aweights[:, columns] = out_tiles[tile]

    for c in range(count):
        for step in range(1, GROUPS):
            a_copy(c, step).wait_send()
            e_copy(c, step).wait_send()

        def drain(k, carry):
            @pl.when(jnp.logical_not(is_me(owner(k))))
            def _():
                b_copy(c, k).wait_send()

            @pl.when(jnp.logical_not(is_me(hub(k))))
            def _():
                d_copy(c, k).wait_send()

            return carry

        def drain_relay(w, carry):
            @pl.when(jnp.logical_not(is_me(relay_to(w))))
            def _():
                r_copy(c, w).wait_send()

            return carry

        lax.fori_loop(0, OWNERS, drain, 0)
        lax.fori_loop(0, 4, drain_relay, 0)


def local(mlp_deltas, mlp_master, mlp_momentum, attn_deltas, attn_master, attn_momentum):
    x, ax = mlp_deltas[0], attn_deltas[0]
    rows = x.shape[1]
    f32, bf16 = jnp.float32, jnp.bfloat16
    scratch = [
        pltpu.VMEM((TILES, rows, LANES), bf16),
        pltpu.VMEM((GROUPS, PART, rows, LANES), bf16),
        pltpu.VMEM((PART, rows, LANES), f32),
        pltpu.VMEM((TILES, rows, LANES), bf16),
    ]
    for _, n in CHUNKS:
        shape = (OWNERS, chunk_rows(n), LANES)
        for kind in (f32, bf16, bf16, f32, f32, bf16, bf16):
            scratch.append(pltpu.VMEM(shape, kind))
    count = len(CHUNKS)
    DMA = pltpu.SemaphoreType.DMA
    scratch += [
        DMA((count, GROUPS)), DMA((count, GROUPS)),
        DMA((count, OWNERS)), DMA((count, OWNERS)),
        DMA((count, OWNERS)), DMA((count, OWNERS)),
        DMA((count, 4)), DMA((count, 4)),
        DMA((count, GROUPS)), DMA((count, GROUPS)),
        DMA(()),
    ]
    shapes = [
        jax.ShapeDtypeStruct(mlp_master.shape, f32),
        jax.ShapeDtypeStruct(mlp_momentum.shape, f32),
        jax.ShapeDtypeStruct(x.shape, bf16),
        jax.ShapeDtypeStruct(attn_master.shape, f32),
        jax.ShapeDtypeStruct(attn_momentum.shape, f32),
        jax.ShapeDtypeStruct(ax.shape, bf16),
    ]
    vmem = pl.BlockSpec(memory_space=pltpu.VMEM)
    return pl.pallas_call(
        kernel,
        out_shape=shapes,
        in_specs=[vmem] * 6,
        out_specs=[vmem] * 6,
        scratch_shapes=scratch,
        compiler_params=pltpu.CompilerParams(collective_id=0, has_side_effects=True),
    )(x, mlp_master, mlp_momentum, ax, attn_master, attn_momentum)


def solution(mesh):
    owned = P(None, ("group", "shard", "tensor"), None)
    attn_owned = P(("group", "shard", "tensor"), None)
    return jax.shard_map(
        local,
        mesh=mesh,
        in_specs=(
            P("group", None, "shard", "tensor"), owned, owned,
            P("group", "shard", "tensor"), attn_owned, attn_owned,
        ),
        out_specs=(
            owned, owned, P(None, "shard", "tensor"),
            attn_owned, attn_owned, P("shard", "tensor"),
        ),
        check_vma=False,
    )
```

```python
import functools

import jax
import jax.numpy as jnp
from jax import lax
from jax.experimental import pallas as pl
from jax.experimental.pallas import tpu as pltpu
from jax.sharding import PartitionSpec as P

momentum_decay = 0.9
outer_rate = 0.7

LANES = 128
UNIT = 5
GROUPS = 4
TENSORS = 4
OWNERS = 16
MLP_TILES = 13
ATTN_TILES = 5
TILES = 3 * MLP_TILES + ATTN_TILES
PART = TILES // GROUPS
CHUNKS = ((0, 3), (3, 8))
MESH = pl.DeviceIdType.MESH


def chunk_rows(count):
    return -(-UNIT * count // 8) * 8


def tile_place(tile):
    if tile < 3 * MLP_TILES:
        return tile // MLP_TILES, tile % MLP_TILES
    return 3, tile - 3 * MLP_TILES


def tile_width(tile):
    matrix, column = tile_place(tile)
    return 64 if matrix < 3 and column == MLP_TILES - 1 else LANES


def remote(src, dst, send_sem, recv_sem, device):
    return pltpu.make_async_remote_copy(
        src_ref=src, dst_ref=dst, send_sem=send_sem, recv_sem=recv_sem,
        device_id=device, device_id_type=MESH,
    )


def kernel(
    *args,
):
    ins, outs, in_vmem, out_vmem, rest = args[0:6], args[6:12], args[12:18], args[18:24], args[24:]
    x_ref, master_ref, mom_ref, ax_ref, amaster_ref, amom_ref = in_vmem
    new_master, new_mom, weights, new_amaster, new_amom, aweights = out_vmem
    tiles, sums, total, out_tiles, *rest = rest
    count = len(CHUNKS)
    per_chunk, sems = rest[: 7 * count], rest[7 * count:]
    stage = per_chunk[0::7]
    sum_send = per_chunk[1::7]
    sum_recv = per_chunk[2::7]
    held_master = per_chunk[3::7]
    held_mom = per_chunk[4::7]
    weight_recv = per_chunk[5::7]
    relay = per_chunk[6::7]
    (a_send, a_recv, b_send, b_recv, d_send, d_recv, r_send, r_recv, e_send, e_recv, local_sem, in_sem, out_sem) = sems

    g = lax.axis_index("group")
    s = lax.axis_index("shard")
    t = lax.axis_index("tensor")
    my_owner = lax.rem(s, 4) * 4 + t

    def peer(step):
        return (lax.rem(g + step, GROUPS), s, t)

    def owner(k):
        return (s // 8, 4 * lax.rem(s, 8) + k // 4, lax.rem(k, 4))

    def trainer(p):
        return (p // 4, g * 8 + s // 4, lax.rem(p, 4))

    x_hi, z = s // 16, lax.rem(s, 16)

    def hub(p):
        return (p // 4, 16 * (g // 2) + z, lax.rem(p, 4))

    def hub_source(slot):
        return (2 * x_hi + slot // 8, 16 * lax.rem(slot // 4, 2) + z, lax.rem(slot, 4))

    def relay_to(w):
        return (g, 16 * x_hi + 4 * w + z // 4, t)

    def relay_source(j):
        return (g, 16 * x_hi + 4 * lax.rem(z, 4) + j, t)

    def is_me(device):
        return (device[0] == g) & (device[1] == s) & (device[2] == t)

    def unless_me(device, action):
        pl.when(jnp.logical_not(is_me(device)))(action)

    loads = [pltpu.make_async_copy(ins[i], in_vmem[i], in_sem.at[i]) for i in range(6)]
    stores = [pltpu.make_async_copy(out_vmem[i], outs[i], out_sem.at[i]) for i in range(6)]
    for i in (0, 3, 1, 2, 4, 5):
        loads[i].start()

    barrier = pltpu.get_barrier_semaphore()

    def greet(device):
        pl.semaphore_signal(barrier, inc=1, device_id=device, device_id_type=MESH)

    def greet_senders(k, carry):
        unless_me(trainer(k), lambda: greet(trainer(k)))
        unless_me(hub_source(k), lambda: greet(hub_source(k)))
        return carry

    def greet_relays(j, carry):
        unless_me(relay_source(j), lambda: greet(relay_source(j)))
        return carry

    for step in range(1, GROUPS):
        greet(peer(step))
    lax.fori_loop(0, OWNERS, greet_senders, 0)
    lax.fori_loop(0, 4, greet_relays, 0)
    own_slot = 4 * (2 * lax.rem(g, 2) + x_hi) + t
    waits = (
        GROUPS - 1 + 2 * OWNERS + 4
        - is_me(owner(my_owner)).astype(jnp.int32)
        - is_me(hub(GROUPS * g + t)).astype(jnp.int32)
        - is_me(relay_to(z // 4)).astype(jnp.int32)
    )

    loads[0].wait()
    loads[3].wait()
    for tile in range(TILES):
        matrix, column = tile_place(tile)
        width = tile_width(tile)
        columns = slice(LANES * column, LANES * column + width)
        block = x_ref[matrix, :, columns] if matrix < 3 else ax_ref[:, columns]
        tiles[tile, :, 0:width] = block

    pl.semaphore_wait(barrier, waits)

    def a_copy(c, step):
        q0, n = CHUNKS[c]
        to = lax.rem(g + step, GROUPS)
        return remote(
            tiles.at[pl.ds(PART * to + q0, n)], sums.at[g, pl.ds(q0, n)],
            a_send.at[c, step], a_recv.at[c, g], peer(step),
        )

    def a_arrival(c, step):
        q0, n = CHUNKS[c]
        source = lax.rem(g + step, GROUPS)
        return remote(
            sums.at[source, pl.ds(q0, n)], sums.at[source, pl.ds(q0, n)],
            a_send.at[c, step], a_recv.at[c, source], peer(step),
        )

    for c in range(count):
        for step in (2, 1, 3):
            a_copy(c, step).start()

    for i in (1, 2, 4, 5):
        loads[i].wait()
    for c, (q0, n) in enumerate(CHUNKS):
        for part in range(GROUPS):
            for q in range(n):
                tile = PART * part + q0 + q
                matrix, column = tile_place(tile)
                width = tile_width(tile)
                for piece in range(TENSORS):
                    slot = part * TENSORS + piece
                    rows = slice(UNIT * q, UNIT * q + UNIT)
                    for held, mlp, attn in (
                        (held_master[c], master_ref, amaster_ref), (held_mom[c], mom_ref, amom_ref),
                    ):
                        if matrix < 3:
                            start = 1600 * piece + LANES * column
                            held[slot, rows, 0:width] = mlp[:, matrix, start:start + width]
                        else:
                            start = 640 * piece + LANES * column
                            held[slot, rows, :] = attn[:, start:start + width]

    def b_copy(c, k):
        return remote(
            sum_send[c].at[k], sum_recv[c].at[g * TENSORS + t],
            b_send.at[c, k], b_recv.at[c, g * TENSORS + t], owner(k),
        )

    def d_copy(c, p):
        return remote(
            sum_recv[c].at[p], relay[c].at[own_slot],
            d_send.at[c, p], d_recv.at[c, own_slot], hub(p),
        )

    def r_copy(c, w):
        bundle = pl.ds(4 * lax.rem(z, 4), 4)
        return remote(
            relay[c].at[pl.ds(4 * w, 4)], weight_recv[c].at[bundle],
            r_send.at[c, w], r_recv.at[c, lax.rem(z, 4)], relay_to(w),
        )

    for c, (q0, n) in enumerate(CHUNKS):
        for step in range(1, GROUPS):
            a_arrival(c, step).wait_recv()
        sources = [lax.rem(g + step, GROUPS) for step in range(1, GROUPS)]
        for q in range(q0, q0 + n):
            value = tiles[PART * g + q].astype(jnp.float32)
            for source in sources:
                value = value + sums[source, q].astype(jnp.float32)
            total[q] = value
        for k in range(OWNERS):
            for q in range(n):
                stage[c][k, UNIT * q:UNIT * q + UNIT, :] = total[q0 + q, UNIT * k:UNIT * k + UNIT, :]

        def hand_out(k, carry):
            sum_send[c][k] = stage[c][k].astype(jnp.bfloat16)
            mine = is_me(owner(k))

            @pl.when(jnp.logical_not(mine))
            def _():
                b_copy(c, k).start()

            @pl.when(mine)
            def _():
                here = pltpu.make_async_copy(
                    sum_send[c].at[k], sum_recv[c].at[g * TENSORS + t], local_sem
                )
                here.start()
                here.wait()

            return carry

        lax.fori_loop(0, OWNERS, hand_out, 0)

    for c in range(count):

        def step_rows(p, carry):
            mine = is_me(trainer(p))

            @pl.when(jnp.logical_not(mine))
            def _():
                remote(
                    sum_recv[c].at[p], sum_recv[c].at[p], b_send.at[c, p], b_recv.at[c, p], trainer(p)
                ).wait_recv()

            grad = sum_recv[c][p].astype(jnp.float32) / GROUPS
            momentum = momentum_decay * held_mom[c][p] + grad
            master = held_master[c][p] - outer_rate * (grad + momentum_decay * momentum)
            held_mom[c][p] = momentum
            held_master[c][p] = master
            sum_recv[c][p] = master.astype(jnp.bfloat16)

            to_me = is_me(hub(p))

            @pl.when(jnp.logical_not(to_me))
            def _():
                d_copy(c, p).start()

            @pl.when(to_me)
            def _():
                here = pltpu.make_async_copy(
                    sum_recv[c].at[p], relay[c].at[own_slot], local_sem
                )
                here.start()
                here.wait()

            return carry

        lax.fori_loop(0, OWNERS, step_rows, 0)

    for c in range(count):

        def pass_on(w, carry):
            for piece in range(TENSORS):
                slot = 4 * w + piece

                @pl.when(jnp.logical_not(is_me(hub_source(slot))))
                def _():
                    remote(
                        relay[c].at[slot], relay[c].at[slot],
                        d_send.at[c, slot], d_recv.at[c, slot], hub_source(slot),
                    ).wait_recv()

            mine = is_me(relay_to(w))

            @pl.when(jnp.logical_not(mine))
            def _():
                r_copy(c, w).start()

            @pl.when(mine)
            def _():
                here = pltpu.make_async_copy(
                    relay[c].at[pl.ds(4 * w, 4)],
                    weight_recv[c].at[pl.ds(4 * lax.rem(z, 4), 4)], local_sem,
                )
                here.start()
                here.wait()

            return carry

        lax.fori_loop(0, 4, pass_on, 0)

    for c, (q0, n) in enumerate(CHUNKS):
        for part in range(GROUPS):
            for q in range(n):
                tile = PART * part + q0 + q
                matrix, column = tile_place(tile)
                width = tile_width(tile)
                for piece in range(TENSORS):
                    slot = part * TENSORS + piece
                    rows = slice(UNIT * q, UNIT * q + UNIT)
                    for held, mlp, attn in (
                        (held_master[c], new_master, new_amaster), (held_mom[c], new_mom, new_amom),
                    ):
                        if matrix < 3:
                            start = 1600 * piece + LANES * column
                            mlp[:, matrix, start:start + width] = held[slot, rows, 0:width]
                        else:
                            start = 640 * piece + LANES * column
                            attn[:, start:start + width] = held[slot, rows, :]

    for i in (0, 1, 3, 4):
        stores[i].start()

    def e_copy(c, step):
        q0, n = CHUNKS[c]
        part = out_tiles.at[pl.ds(PART * g + q0, n)]
        return remote(part, part, e_send.at[c, step], e_recv.at[c, g], peer(step))

    def e_arrival(c, step):
        q0, n = CHUNKS[c]
        source = lax.rem(g + step, GROUPS)
        part = out_tiles.at[pl.ds(PART * source + q0, n)]
        return remote(part, part, e_send.at[c, step], e_recv.at[c, source], peer(step))

    for c, (q0, n) in enumerate(CHUNKS):

        def take_in(j, carry):
            bundle = weight_recv[c].at[pl.ds(4 * j, 4)]

            @pl.when(jnp.logical_not(is_me(relay_source(j))))
            def _():
                remote(
                    bundle, bundle, r_send.at[c, j], r_recv.at[c, j], relay_source(j)
                ).wait_recv()

            for piece in range(TENSORS):
                stage[c][4 * j + piece] = weight_recv[c][4 * j + piece].astype(jnp.float32)
            return carry

        lax.fori_loop(0, 4, take_in, 0)
        for k in range(OWNERS):
            for q in range(n):
                total[q0 + q, UNIT * k:UNIT * k + UNIT, :] = stage[c][k, UNIT * q:UNIT * q + UNIT, :]
        for q in range(q0, q0 + n):
            out_tiles[PART * g + q] = total[q].astype(jnp.bfloat16)
        for step in (2, 1, 3):
            e_copy(c, step).start()

    for c in range(count):
        for step in range(1, GROUPS):
            e_arrival(c, step).wait_recv()
    for tile in range(TILES):
        matrix, column = tile_place(tile)
        width = tile_width(tile)
        columns = slice(LANES * column, LANES * column + width)
        if matrix < 3:
            weights[matrix, :, columns] = out_tiles[tile, :, 0:width]
        else:
            aweights[:, columns] = out_tiles[tile]
    for i in (2, 5):
        stores[i].start()

    for c in range(count):
        for step in range(1, GROUPS):
            a_copy(c, step).wait_send()
            e_copy(c, step).wait_send()

        def drain(k, carry):
            @pl.when(jnp.logical_not(is_me(owner(k))))
            def _():
                b_copy(c, k).wait_send()

            @pl.when(jnp.logical_not(is_me(hub(k))))
            def _():
                d_copy(c, k).wait_send()

            return carry

        def drain_relay(w, carry):
            @pl.when(jnp.logical_not(is_me(relay_to(w))))
            def _():
                r_copy(c, w).wait_send()

            return carry

        lax.fori_loop(0, OWNERS, drain, 0)
        lax.fori_loop(0, 4, drain_relay, 0)
    for store in stores:
        store.wait()


def finish(*args):
    ins, outs, held, (in_sem, out_sem) = args[0:6], args[6:12], args[12:18], args[18:20]
    loads = [pltpu.make_async_copy(ins[i], held[i], in_sem.at[i]) for i in range(6)]
    stores = [pltpu.make_async_copy(held[i], outs[i], out_sem.at[i]) for i in range(6)]
    for load in loads:
        load.start()
    for load, store in zip(loads, stores):
        load.wait()
        store.start()
    for store in stores:
        store.wait()


def local(mlp_deltas, mlp_master, mlp_momentum, attn_deltas, attn_master, attn_momentum):
    x, ax = mlp_deltas[0], attn_deltas[0]
    mlp_master, mlp_momentum = (a.transpose(1, 0, 2) for a in (mlp_master, mlp_momentum))
    rows = x.shape[1]
    f32, bf16 = jnp.float32, jnp.bfloat16
    ins = (x, mlp_master, mlp_momentum, ax, attn_master, attn_momentum)
    outs = (mlp_master, mlp_momentum, x, attn_master, attn_momentum, ax)
    scratch = [pltpu.VMEM(a.shape, a.dtype) for a in ins + outs]
    scratch += [
        pltpu.VMEM((TILES, rows, LANES), bf16),
        pltpu.VMEM((GROUPS, PART, rows, LANES), bf16),
        pltpu.VMEM((PART, rows, LANES), f32),
        pltpu.VMEM((TILES, rows, LANES), bf16),
    ]
    for _, n in CHUNKS:
        shape = (OWNERS, chunk_rows(n), LANES)
        for kind in (f32, bf16, bf16, f32, f32, bf16, bf16):
            scratch.append(pltpu.VMEM(shape, kind))
    count = len(CHUNKS)
    DMA = pltpu.SemaphoreType.DMA
    scratch += [
        DMA((count, GROUPS)), DMA((count, GROUPS)),
        DMA((count, OWNERS)), DMA((count, OWNERS)),
        DMA((count, OWNERS)), DMA((count, OWNERS)),
        DMA((count, 4)), DMA((count, 4)),
        DMA((count, GROUPS)), DMA((count, GROUPS)),
        DMA(()), DMA((6,)), DMA((6,)),
    ]
    shapes = [jax.ShapeDtypeStruct(a.shape, a.dtype) for a in outs]
    anywhere = [pl.BlockSpec(memory_space=pl.ANY)] * 6
    results = pl.pallas_call(
        kernel,
        out_shape=shapes,
        in_specs=anywhere,
        out_specs=anywhere,
        scratch_shapes=scratch,
        compiler_params=pltpu.CompilerParams(collective_id=0, has_side_effects=True),
    )(*ins)
    master, momentum, weights, amaster, amomentum, aweights = pl.pallas_call(
        finish,
        out_shape=shapes,
        in_specs=anywhere,
        out_specs=anywhere,
        scratch_shapes=[pltpu.VMEM(a.shape, a.dtype) for a in outs] + [DMA((6,)), DMA((6,))],
    )(*results)
    return (
        master.transpose(1, 0, 2), momentum.transpose(1, 0, 2), weights,
        amaster, amomentum, aweights,
    )


def solution(mesh):
    owned = P(None, ("group", "shard", "tensor"), None)
    attn_owned = P(("group", "shard", "tensor"), None)
    return jax.shard_map(
        local,
        mesh=mesh,
        in_specs=(
            P("group", None, "shard", "tensor"), owned, owned,
            P("group", "shard", "tensor"), attn_owned, attn_owned,
        ),
        out_specs=(
            owned, owned, P(None, "shard", "tensor"),
            attn_owned, attn_owned, P("shard", "tensor"),
        ),
        check_vma=False,
    )
```

```python
import functools

import jax
import jax.numpy as jnp
from jax import lax
from jax.experimental import pallas as pl
from jax.experimental.pallas import tpu as pltpu
from jax.sharding import PartitionSpec as P

momentum_decay = 0.9
outer_rate = 0.7

LANES = 128
UNIT = 5
GROUPS = 4
TENSORS = 4
OWNERS = 16
MLP_TILES = 13
ATTN_TILES = 5
TILES = 3 * MLP_TILES + ATTN_TILES
PART = TILES // GROUPS
CHUNKS = ((0, 3), (3, 3), (6, 5))
MESH = pl.DeviceIdType.MESH


def chunk_rows(count):
    return -(-UNIT * count // 8) * 8


def tile_place(tile):
    if tile < 3 * MLP_TILES:
        return tile // MLP_TILES, tile % MLP_TILES
    return 3, tile - 3 * MLP_TILES


def tile_width(tile):
    matrix, column = tile_place(tile)
    return 64 if matrix < 3 and column == MLP_TILES - 1 else LANES


def remote(src, dst, send_sem, recv_sem, device):
    return pltpu.make_async_remote_copy(
        src_ref=src, dst_ref=dst, send_sem=send_sem, recv_sem=recv_sem,
        device_id=device, device_id_type=MESH,
    )


def kernel(
    *args,
):
    ins, outs, in_vmem, out_vmem, rest = args[0:6], args[6:12], args[12:18], args[18:24], args[24:]
    x_ref, master_ref, mom_ref, ax_ref, amaster_ref, amom_ref = in_vmem
    new_master, new_mom, weights, new_amaster, new_amom, aweights = out_vmem
    tiles, sums, total, out_tiles, *rest = rest
    count = len(CHUNKS)
    per_chunk, sems = rest[: 7 * count], rest[7 * count:]
    stage = per_chunk[0::7]
    sum_send = per_chunk[1::7]
    sum_recv = per_chunk[2::7]
    held_master = per_chunk[3::7]
    held_mom = per_chunk[4::7]
    weight_recv = per_chunk[5::7]
    relay = per_chunk[6::7]
    (a_send, a_recv, b_send, b_recv, d_send, d_recv, r_send, r_recv, e_send, e_recv, local_sem, in_sem, out_sem, near) = sems

    g = lax.axis_index("group")
    s = lax.axis_index("shard")
    t = lax.axis_index("tensor")
    my_owner = lax.rem(s, 4) * 4 + t

    def peer(step):
        return (lax.rem(g + step, GROUPS), s, t)

    def owner(k):
        return (s // 8, 4 * lax.rem(s, 8) + k // 4, lax.rem(k, 4))

    def trainer(p):
        return (p // 4, g * 8 + s // 4, lax.rem(p, 4))

    x_hi, z = s // 16, lax.rem(s, 16)

    def hub(p):
        return (p // 4, 16 * (g // 2) + z, lax.rem(p, 4))

    def hub_source(slot):
        return (2 * x_hi + slot // 8, 16 * lax.rem(slot // 4, 2) + z, lax.rem(slot, 4))

    def relay_to(w):
        return (g, 16 * x_hi + 4 * w + z // 4, t)

    def relay_source(j):
        return (g, 16 * x_hi + 4 * lax.rem(z, 4) + j, t)

    def is_me(device):
        return (device[0] == g) & (device[1] == s) & (device[2] == t)

    def unless_me(device, action):
        pl.when(jnp.logical_not(is_me(device)))(action)

    loads = [pltpu.make_async_copy(ins[i], in_vmem[i], in_sem.at[i]) for i in range(6)]
    stores = [pltpu.make_async_copy(out_vmem[i], outs[i], out_sem.at[i]) for i in range(6)]
    for i in (0, 3, 1, 2, 4, 5):
        loads[i].start()

    barrier = pltpu.get_barrier_semaphore()
    above = (g, 16 * x_hi + lax.rem(z + 1, 16), t)
    below = (g, 16 * x_hi + lax.rem(z + 15, 16), t)

    def greet(device):
        pl.semaphore_signal(barrier, inc=1, device_id=device, device_id_type=MESH)

    def greet_plane(k, carry):
        unless_me(hub(k), lambda: greet(hub(k)))
        unless_me(hub_source(k), lambda: greet(hub_source(k)))
        return carry

    for device in (peer(1), peer(2), peer(3), above, below):
        greet(device)
    lax.fori_loop(0, OWNERS, greet_plane, 0)
    own_slot = 4 * (2 * lax.rem(g, 2) + x_hi) + t
    waits = GROUPS + 1 + 2 * OWNERS - 2 * is_me(hub(GROUPS * g + t)).astype(jnp.int32)

    loads[0].wait()
    loads[3].wait()
    for tile in range(TILES):
        matrix, column = tile_place(tile)
        width = tile_width(tile)
        columns = slice(LANES * column, LANES * column + width)
        block = x_ref[matrix, :, columns] if matrix < 3 else ax_ref[:, columns]
        tiles[tile, :, 0:width] = block

    pl.semaphore_wait(barrier, waits)

    def a_copy(c, step):
        q0, n = CHUNKS[c]
        to = lax.rem(g + step, GROUPS)
        return remote(
            tiles.at[pl.ds(PART * to + q0, n)], sums.at[g, pl.ds(q0, n)],
            a_send.at[c, step], a_recv.at[c, g], peer(step),
        )

    def a_arrival(c, step):
        q0, n = CHUNKS[c]
        source = lax.rem(g + step, GROUPS)
        return remote(
            sums.at[source, pl.ds(q0, n)], sums.at[source, pl.ds(q0, n)],
            a_send.at[c, step], a_recv.at[c, source], peer(step),
        )

    for c in range(count):
        for step in (2, 1, 3):
            a_copy(c, step).start()

    for i in (1, 2, 4, 5):
        loads[i].wait()
    for c, (q0, n) in enumerate(CHUNKS):
        for part in range(GROUPS):
            for q in range(n):
                tile = PART * part + q0 + q
                matrix, column = tile_place(tile)
                width = tile_width(tile)
                for piece in range(TENSORS):
                    slot = part * TENSORS + piece
                    rows = slice(UNIT * q, UNIT * q + UNIT)
                    for held, mlp, attn in (
                        (held_master[c], master_ref, amaster_ref), (held_mom[c], mom_ref, amom_ref),
                    ):
                        if matrix < 3:
                            start = 1600 * piece + LANES * column
                            held[slot, rows, 0:width] = mlp[:, matrix, start:start + width]
                        else:
                            start = 640 * piece + LANES * column
                            held[slot, rows, :] = attn[:, start:start + width]

    def meet(i, carry):
        pl.semaphore_signal(near.at[0], inc=1, device_id=above, device_id_type=MESH)
        pl.semaphore_signal(near.at[1], inc=1, device_id=below, device_id_type=MESH)
        pl.semaphore_wait(near.at[0], 1)
        pl.semaphore_wait(near.at[1], 1)
        return carry

    lax.fori_loop(0, 8, meet, 0)

    def b_copy(c, k):
        return remote(
            sum_send[c].at[k], sum_recv[c].at[g * TENSORS + t],
            b_send.at[c, k], b_recv.at[c, g * TENSORS + t], owner(k),
        )

    def d_copy(c, p):
        return remote(
            sum_recv[c].at[p], relay[c].at[own_slot],
            d_send.at[c, p], d_recv.at[c, own_slot], hub(p),
        )

    def r_copy(c, w):
        bundle = pl.ds(4 * lax.rem(z, 4), 4)
        return remote(
            relay[c].at[pl.ds(4 * w, 4)], weight_recv[c].at[bundle],
            r_send.at[c, w], r_recv.at[c, lax.rem(z, 4)], relay_to(w),
        )

    for c, (q0, n) in enumerate(CHUNKS):
        for step in range(1, GROUPS):
            a_arrival(c, step).wait_recv()
        sources = [lax.rem(g + step, GROUPS) for step in range(1, GROUPS)]
        for q in range(q0, q0 + n):
            value = tiles[PART * g + q].astype(jnp.float32)
            for source in sources:
                value = value + sums[source, q].astype(jnp.float32)
            total[q] = value
        for k in range(OWNERS):
            for q in range(n):
                stage[c][k, UNIT * q:UNIT * q + UNIT, :] = total[q0 + q, UNIT * k:UNIT * k + UNIT, :]

        def hand_out(k, carry):
            sum_send[c][k] = stage[c][k].astype(jnp.bfloat16)
            mine = is_me(owner(k))

            @pl.when(jnp.logical_not(mine))
            def _():
                b_copy(c, k).start()

            @pl.when(mine)
            def _():
                here = pltpu.make_async_copy(
                    sum_send[c].at[k], sum_recv[c].at[g * TENSORS + t], local_sem
                )
                here.start()
                here.wait()

            return carry

        lax.fori_loop(0, OWNERS, hand_out, 0)

    for c in range(count):

        def step_rows(p, carry):
            mine = is_me(trainer(p))

            @pl.when(jnp.logical_not(mine))
            def _():
                remote(
                    sum_recv[c].at[p], sum_recv[c].at[p], b_send.at[c, p], b_recv.at[c, p], trainer(p)
                ).wait_recv()

            grad = sum_recv[c][p].astype(jnp.float32) / GROUPS
            momentum = momentum_decay * held_mom[c][p] + grad
            master = held_master[c][p] - outer_rate * (grad + momentum_decay * momentum)
            held_mom[c][p] = momentum
            held_master[c][p] = master
            sum_recv[c][p] = master.astype(jnp.bfloat16)

            to_me = is_me(hub(p))

            @pl.when(jnp.logical_not(to_me))
            def _():
                d_copy(c, p).start()

            @pl.when(to_me)
            def _():
                here = pltpu.make_async_copy(
                    sum_recv[c].at[p], relay[c].at[own_slot], local_sem
                )
                here.start()
                here.wait()

            return carry

        lax.fori_loop(0, OWNERS, step_rows, 0)

        def pass_on(w, carry):
            for piece in range(TENSORS):
                slot = 4 * w + piece

                @pl.when(jnp.logical_not(is_me(hub_source(slot))))
                def _():
                    remote(
                        relay[c].at[slot], relay[c].at[slot],
                        d_send.at[c, slot], d_recv.at[c, slot], hub_source(slot),
                    ).wait_recv()

            mine = is_me(relay_to(w))

            @pl.when(jnp.logical_not(mine))
            def _():
                r_copy(c, w).start()

            @pl.when(mine)
            def _():
                here = pltpu.make_async_copy(
                    relay[c].at[pl.ds(4 * w, 4)],
                    weight_recv[c].at[pl.ds(4 * lax.rem(z, 4), 4)], local_sem,
                )
                here.start()
                here.wait()

            return carry

        lax.fori_loop(0, 4, pass_on, 0)

    for c, (q0, n) in enumerate(CHUNKS):
        for part in range(GROUPS):
            for q in range(n):
                tile = PART * part + q0 + q
                matrix, column = tile_place(tile)
                width = tile_width(tile)
                for piece in range(TENSORS):
                    slot = part * TENSORS + piece
                    rows = slice(UNIT * q, UNIT * q + UNIT)
                    for held, mlp, attn in (
                        (held_master[c], new_master, new_amaster), (held_mom[c], new_mom, new_amom),
                    ):
                        if matrix < 3:
                            start = 1600 * piece + LANES * column
                            mlp[:, matrix, start:start + width] = held[slot, rows, 0:width]
                        else:
                            start = 640 * piece + LANES * column
                            attn[:, start:start + width] = held[slot, rows, :]

    for i in (0, 1, 3, 4):
        stores[i].start()

    def e_copy(c, step):
        q0, n = CHUNKS[c]
        part = out_tiles.at[pl.ds(PART * g + q0, n)]
        return remote(part, part, e_send.at[c, step], e_recv.at[c, g], peer(step))

    def e_arrival(c, step):
        q0, n = CHUNKS[c]
        source = lax.rem(g + step, GROUPS)
        part = out_tiles.at[pl.ds(PART * source + q0, n)]
        return remote(part, part, e_send.at[c, step], e_recv.at[c, source], peer(step))

    for c, (q0, n) in enumerate(CHUNKS):

        def take_in(j, carry):
            bundle = weight_recv[c].at[pl.ds(4 * j, 4)]

            @pl.when(jnp.logical_not(is_me(relay_source(j))))
            def _():
                remote(
                    bundle, bundle, r_send.at[c, j], r_recv.at[c, j], relay_source(j)
                ).wait_recv()

            for piece in range(TENSORS):
                stage[c][4 * j + piece] = weight_recv[c][4 * j + piece].astype(jnp.float32)
            return carry

        lax.fori_loop(0, 4, take_in, 0)
        for k in range(OWNERS):
            for q in range(n):
                total[q0 + q, UNIT * k:UNIT * k + UNIT, :] = stage[c][k, UNIT * q:UNIT * q + UNIT, :]
        for q in range(q0, q0 + n):
            out_tiles[PART * g + q] = total[q].astype(jnp.bfloat16)
        for step in (2, 1, 3):
            e_copy(c, step).start()

    for c in range(count):
        for step in range(1, GROUPS):
            e_arrival(c, step).wait_recv()
    for tile in range(TILES):
        matrix, column = tile_place(tile)
        width = tile_width(tile)
        columns = slice(LANES * column, LANES * column + width)
        if matrix < 3:
            weights[matrix, :, columns] = out_tiles[tile, :, 0:width]
        else:
            aweights[:, columns] = out_tiles[tile]
    for i in (2, 5):
        stores[i].start()

    for c in range(count):
        for step in range(1, GROUPS):
            a_copy(c, step).wait_send()
            e_copy(c, step).wait_send()

        def drain(k, carry):
            @pl.when(jnp.logical_not(is_me(owner(k))))
            def _():
                b_copy(c, k).wait_send()

            @pl.when(jnp.logical_not(is_me(hub(k))))
            def _():
                d_copy(c, k).wait_send()

            return carry

        def drain_relay(w, carry):
            @pl.when(jnp.logical_not(is_me(relay_to(w))))
            def _():
                r_copy(c, w).wait_send()

            return carry

        lax.fori_loop(0, OWNERS, drain, 0)
        lax.fori_loop(0, 4, drain_relay, 0)
    for store in stores:
        store.wait()


def finish(*args):
    ins, outs, held, (in_sem, out_sem) = args[0:6], args[6:12], args[12:18], args[18:20]
    loads = [pltpu.make_async_copy(ins[i], held[i], in_sem.at[i]) for i in range(6)]
    stores = [pltpu.make_async_copy(held[i], outs[i], out_sem.at[i]) for i in range(6)]
    for load in loads:
        load.start()
    for load, store in zip(loads, stores):
        load.wait()
        store.start()
    for store in stores:
        store.wait()


def local(mlp_deltas, mlp_master, mlp_momentum, attn_deltas, attn_master, attn_momentum):
    x, ax = mlp_deltas[0], attn_deltas[0]
    mlp_master, mlp_momentum = (a.transpose(1, 0, 2) for a in (mlp_master, mlp_momentum))
    rows = x.shape[1]
    f32, bf16 = jnp.float32, jnp.bfloat16
    ins = (x, mlp_master, mlp_momentum, ax, attn_master, attn_momentum)
    outs = (mlp_master, mlp_momentum, x, attn_master, attn_momentum, ax)
    scratch = [pltpu.VMEM(a.shape, a.dtype) for a in ins + outs]
    scratch += [
        pltpu.VMEM((TILES, rows, LANES), bf16),
        pltpu.VMEM((GROUPS, PART, rows, LANES), bf16),
        pltpu.VMEM((PART, rows, LANES), f32),
        pltpu.VMEM((TILES, rows, LANES), bf16),
    ]
    for _, n in CHUNKS:
        shape = (OWNERS, chunk_rows(n), LANES)
        for kind in (f32, bf16, bf16, f32, f32, bf16, bf16):
            scratch.append(pltpu.VMEM(shape, kind))
    count = len(CHUNKS)
    DMA = pltpu.SemaphoreType.DMA
    scratch += [
        DMA((count, GROUPS)), DMA((count, GROUPS)),
        DMA((count, OWNERS)), DMA((count, OWNERS)),
        DMA((count, OWNERS)), DMA((count, OWNERS)),
        DMA((count, 4)), DMA((count, 4)),
        DMA((count, GROUPS)), DMA((count, GROUPS)),
        DMA(()), DMA((6,)), DMA((6,)), pltpu.SemaphoreType.REGULAR((2,)),
    ]
    shapes = [jax.ShapeDtypeStruct(a.shape, a.dtype) for a in outs]
    anywhere = [pl.BlockSpec(memory_space=pl.ANY)] * 6
    results = pl.pallas_call(
        kernel,
        out_shape=shapes,
        in_specs=anywhere,
        out_specs=anywhere,
        scratch_shapes=scratch,
        compiler_params=pltpu.CompilerParams(collective_id=0, has_side_effects=True),
    )(*ins)
    master, momentum, weights, amaster, amomentum, aweights = pl.pallas_call(
        finish,
        out_shape=shapes,
        in_specs=anywhere,
        out_specs=anywhere,
        scratch_shapes=[pltpu.VMEM(a.shape, a.dtype) for a in outs] + [DMA((6,)), DMA((6,))],
    )(*results)
    return (
        master.transpose(1, 0, 2), momentum.transpose(1, 0, 2), weights,
        amaster, amomentum, aweights,
    )


def solution(mesh):
    owned = P(None, ("group", "shard", "tensor"), None)
    attn_owned = P(("group", "shard", "tensor"), None)
    return jax.shard_map(
        local,
        mesh=mesh,
        in_specs=(
            P("group", None, "shard", "tensor"), owned, owned,
            P("group", "shard", "tensor"), attn_owned, attn_owned,
        ),
        out_specs=(
            owned, owned, P(None, "shard", "tensor"),
            attn_owned, attn_owned, P("shard", "tensor"),
        ),
        check_vma=False,
    )
```

```python
import functools

import jax
import jax.numpy as jnp
from jax import lax
from jax.experimental import pallas as pl
from jax.experimental.pallas import tpu as pltpu
from jax.sharding import PartitionSpec as P

momentum_decay = 0.9
outer_rate = 0.7

LANES = 128
UNIT = 5
GROUPS = 4
TENSORS = 4
OWNERS = 16
MLP_TILES = 13
ATTN_TILES = 5
TILES = 3 * MLP_TILES + ATTN_TILES
PART = TILES // GROUPS
CHUNKS = ((0, 3), (3, 3), (6, 5))
MESH = pl.DeviceIdType.MESH


def chunk_rows(count):
    return -(-UNIT * count // 8) * 8


def tile_place(tile):
    if tile < 3 * MLP_TILES:
        return tile // MLP_TILES, tile % MLP_TILES
    return 3, tile - 3 * MLP_TILES


def tile_width(tile):
    matrix, column = tile_place(tile)
    return 64 if matrix < 3 and column == MLP_TILES - 1 else LANES


def remote(src, dst, send_sem, recv_sem, device):
    return pltpu.make_async_remote_copy(
        src_ref=src, dst_ref=dst, send_sem=send_sem, recv_sem=recv_sem,
        device_id=device, device_id_type=MESH,
    )


def kernel(
    *args,
):
    ins, outs, in_vmem, out_vmem, rest = args[0:6], args[6:11], args[11:17], args[17:21], args[21:]
    x_ref, master_ref, mom_ref, ax_ref, amaster_ref, amom_ref = in_vmem
    new_master, new_mom, new_amaster, new_amom = out_vmem
    landed = outs[4]
    tiles, sums, total, out_tiles, *rest = rest
    count = len(CHUNKS)
    per_chunk, sems = rest[: 7 * count], rest[7 * count:]
    stage = per_chunk[0::7]
    sum_send = per_chunk[1::7]
    sum_recv = per_chunk[2::7]
    held_master = per_chunk[3::7]
    held_mom = per_chunk[4::7]
    weight_recv = per_chunk[5::7]
    relay = per_chunk[6::7]
    (a_send, a_recv, b_send, b_recv, d_send, d_recv, r_send, r_recv, e_send, e_recv, local_sem, in_sem, out_sem) = sems

    g = lax.axis_index("group")
    s = lax.axis_index("shard")
    t = lax.axis_index("tensor")
    my_owner = lax.rem(s, 4) * 4 + t

    def peer(step):
        return (lax.rem(g + step, GROUPS), s, t)

    def owner(k):
        return (s // 8, 4 * lax.rem(s, 8) + k // 4, lax.rem(k, 4))

    def trainer(p):
        return (p // 4, g * 8 + s // 4, lax.rem(p, 4))

    x_hi, z = s // 16, lax.rem(s, 16)

    def hub(p):
        return (p // 4, 16 * (g // 2) + z, lax.rem(p, 4))

    def hub_source(slot):
        return (2 * x_hi + slot // 8, 16 * lax.rem(slot // 4, 2) + z, lax.rem(slot, 4))

    def relay_to(w):
        return (g, 16 * x_hi + 4 * w + z // 4, t)

    def relay_source(j):
        return (g, 16 * x_hi + 4 * lax.rem(z, 4) + j, t)

    def is_me(device):
        return (device[0] == g) & (device[1] == s) & (device[2] == t)

    def unless_me(device, action):
        pl.when(jnp.logical_not(is_me(device)))(action)

    loads = [pltpu.make_async_copy(ins[i], in_vmem[i], in_sem.at[i]) for i in range(6)]
    stores = [pltpu.make_async_copy(out_vmem[i], outs[i], out_sem.at[i]) for i in range(4)]
    for i in (0, 3, 1, 2, 4, 5):
        loads[i].start()

    barrier = pltpu.get_barrier_semaphore()

    def greet(device):
        pl.semaphore_signal(barrier, inc=1, device_id=device, device_id_type=MESH)

    def greet_senders(k, carry):
        unless_me(trainer(k), lambda: greet(trainer(k)))
        unless_me(hub_source(k), lambda: greet(hub_source(k)))
        return carry

    def greet_relays(j, carry):
        unless_me(relay_source(j), lambda: greet(relay_source(j)))
        return carry

    for step in range(1, GROUPS):
        greet(peer(step))
    lax.fori_loop(0, OWNERS, greet_senders, 0)
    lax.fori_loop(0, 4, greet_relays, 0)
    own_slot = 4 * (2 * lax.rem(g, 2) + x_hi) + t
    waits = (
        GROUPS - 1 + 2 * OWNERS + 4
        - is_me(owner(my_owner)).astype(jnp.int32)
        - is_me(hub(GROUPS * g + t)).astype(jnp.int32)
        - is_me(relay_to(z // 4)).astype(jnp.int32)
    )

    loads[0].wait()
    loads[3].wait()
    for tile in range(TILES):
        matrix, column = tile_place(tile)
        width = tile_width(tile)
        columns = slice(LANES * column, LANES * column + width)
        block = x_ref[matrix, :, columns] if matrix < 3 else ax_ref[:, columns]
        tiles[tile, :, 0:width] = block

    pl.semaphore_wait(barrier, waits)

    def a_copy(c, step):
        q0, n = CHUNKS[c]
        to = lax.rem(g + step, GROUPS)
        return remote(
            tiles.at[pl.ds(PART * to + q0, n)], sums.at[g, pl.ds(q0, n)],
            a_send.at[c, step], a_recv.at[c, g], peer(step),
        )

    def a_arrival(c, step):
        q0, n = CHUNKS[c]
        source = lax.rem(g + step, GROUPS)
        return remote(
            sums.at[source, pl.ds(q0, n)], sums.at[source, pl.ds(q0, n)],
            a_send.at[c, step], a_recv.at[c, source], peer(step),
        )

    for c in range(count):
        for step in (2, 1, 3):
            a_copy(c, step).start()

    for i in (1, 2, 4, 5):
        loads[i].wait()
    for c, (q0, n) in enumerate(CHUNKS):
        for part in range(GROUPS):
            for q in range(n):
                tile = PART * part + q0 + q
                matrix, column = tile_place(tile)
                width = tile_width(tile)
                for piece in range(TENSORS):
                    slot = part * TENSORS + piece
                    rows = slice(UNIT * q, UNIT * q + UNIT)
                    for held, mlp, attn in (
                        (held_master[c], master_ref, amaster_ref), (held_mom[c], mom_ref, amom_ref),
                    ):
                        if matrix < 3:
                            start = 1600 * piece + LANES * column
                            held[slot, rows, 0:width] = mlp[:, matrix, start:start + width]
                        else:
                            start = 640 * piece + LANES * column
                            held[slot, rows, :] = attn[:, start:start + width]

    def b_copy(c, k):
        return remote(
            sum_send[c].at[k], sum_recv[c].at[g * TENSORS + t],
            b_send.at[c, k], b_recv.at[c, g * TENSORS + t], owner(k),
        )

    def d_copy(c, p):
        return remote(
            sum_recv[c].at[p], relay[c].at[own_slot],
            d_send.at[c, p], d_recv.at[c, own_slot], hub(p),
        )

    def r_copy(c, w):
        bundle = pl.ds(4 * lax.rem(z, 4), 4)
        return remote(
            relay[c].at[pl.ds(4 * w, 4)], weight_recv[c].at[bundle],
            r_send.at[c, w], r_recv.at[c, lax.rem(z, 4)], relay_to(w),
        )

    for c, (q0, n) in enumerate(CHUNKS):
        for step in range(1, GROUPS):
            a_arrival(c, step).wait_recv()
        sources = [lax.rem(g + step, GROUPS) for step in range(1, GROUPS)]
        for q in range(q0, q0 + n):
            value = tiles[PART * g + q].astype(jnp.float32)
            for source in sources:
                value = value + sums[source, q].astype(jnp.float32)
            total[q] = value
        for k in range(OWNERS):
            for q in range(n):
                stage[c][k, UNIT * q:UNIT * q + UNIT, :] = total[q0 + q, UNIT * k:UNIT * k + UNIT, :]

        def hand_out(k, carry):
            sum_send[c][k] = stage[c][k].astype(jnp.bfloat16)
            mine = is_me(owner(k))

            @pl.when(jnp.logical_not(mine))
            def _():
                b_copy(c, k).start()

            @pl.when(mine)
            def _():
                here = pltpu.make_async_copy(
                    sum_send[c].at[k], sum_recv[c].at[g * TENSORS + t], local_sem
                )
                here.start()
                here.wait()

            return carry

        lax.fori_loop(0, OWNERS, hand_out, 0)

    for c in range(count):

        def step_rows(p, carry):
            mine = is_me(trainer(p))

            @pl.when(jnp.logical_not(mine))
            def _():
                remote(
                    sum_recv[c].at[p], sum_recv[c].at[p], b_send.at[c, p], b_recv.at[c, p], trainer(p)
                ).wait_recv()

            grad = sum_recv[c][p].astype(jnp.float32) / GROUPS
            momentum = momentum_decay * held_mom[c][p] + grad
            master = held_master[c][p] - outer_rate * (grad + momentum_decay * momentum)
            held_mom[c][p] = momentum
            held_master[c][p] = master
            sum_recv[c][p] = master.astype(jnp.bfloat16)

            to_me = is_me(hub(p))

            @pl.when(jnp.logical_not(to_me))
            def _():
                d_copy(c, p).start()

            @pl.when(to_me)
            def _():
                here = pltpu.make_async_copy(
                    sum_recv[c].at[p], relay[c].at[own_slot], local_sem
                )
                here.start()
                here.wait()

            return carry

        lax.fori_loop(0, OWNERS, step_rows, 0)

        def pass_on(w, carry):
            for piece in range(TENSORS):
                slot = 4 * w + piece

                @pl.when(jnp.logical_not(is_me(hub_source(slot))))
                def _():
                    remote(
                        relay[c].at[slot], relay[c].at[slot],
                        d_send.at[c, slot], d_recv.at[c, slot], hub_source(slot),
                    ).wait_recv()

            mine = is_me(relay_to(w))

            @pl.when(jnp.logical_not(mine))
            def _():
                r_copy(c, w).start()

            @pl.when(mine)
            def _():
                here = pltpu.make_async_copy(
                    relay[c].at[pl.ds(4 * w, 4)],
                    weight_recv[c].at[pl.ds(4 * lax.rem(z, 4), 4)], local_sem,
                )
                here.start()
                here.wait()

            return carry

        lax.fori_loop(0, 4, pass_on, 0)

    for c, (q0, n) in enumerate(CHUNKS):
        for part in range(GROUPS):
            for q in range(n):
                tile = PART * part + q0 + q
                matrix, column = tile_place(tile)
                width = tile_width(tile)
                for piece in range(TENSORS):
                    slot = part * TENSORS + piece
                    rows = slice(UNIT * q, UNIT * q + UNIT)
                    for held, mlp, attn in (
                        (held_master[c], new_master, new_amaster), (held_mom[c], new_mom, new_amom),
                    ):
                        if matrix < 3:
                            start = 1600 * piece + LANES * column
                            mlp[:, matrix, start:start + width] = held[slot, rows, 0:width]
                        else:
                            start = 640 * piece + LANES * column
                            attn[:, start:start + width] = held[slot, rows, :]

    for store in stores:
        store.start()

    def e_copy(c, step):
        q0, n = CHUNKS[c]
        part = pl.ds(PART * g + q0, n)
        return remote(out_tiles.at[part], landed.at[part], e_send.at[c, step], e_recv.at[c, g], peer(step))

    def e_arrival(c, step):
        q0, n = CHUNKS[c]
        source = lax.rem(g + step, GROUPS)
        part = landed.at[pl.ds(PART * source + q0, n)]
        return remote(part, part, e_send.at[c, step], e_recv.at[c, source], peer(step))

    for c, (q0, n) in enumerate(CHUNKS):

        def take_in(j, carry):
            bundle = weight_recv[c].at[pl.ds(4 * j, 4)]

            @pl.when(jnp.logical_not(is_me(relay_source(j))))
            def _():
                remote(
                    bundle, bundle, r_send.at[c, j], r_recv.at[c, j], relay_source(j)
                ).wait_recv()

            for piece in range(TENSORS):
                stage[c][4 * j + piece] = weight_recv[c][4 * j + piece].astype(jnp.float32)
            return carry

        lax.fori_loop(0, 4, take_in, 0)
        for k in range(OWNERS):
            for q in range(n):
                total[q0 + q, UNIT * k:UNIT * k + UNIT, :] = stage[c][k, UNIT * q:UNIT * q + UNIT, :]
        for q in range(q0, q0 + n):
            out_tiles[PART * g + q] = total[q].astype(jnp.bfloat16)
        for step in (2, 1, 3):
            e_copy(c, step).start()
        part = pl.ds(PART * g + q0, n)
        stores.append(pltpu.make_async_copy(out_tiles.at[part], landed.at[part], out_sem.at[4 + c]))
        stores[-1].start()

    for c in range(count):
        for step in range(1, GROUPS):
            e_arrival(c, step).wait_recv()

    for c in range(count):
        for step in range(1, GROUPS):
            a_copy(c, step).wait_send()
            e_copy(c, step).wait_send()

        def drain(k, carry):
            @pl.when(jnp.logical_not(is_me(owner(k))))
            def _():
                b_copy(c, k).wait_send()

            @pl.when(jnp.logical_not(is_me(hub(k))))
            def _():
                d_copy(c, k).wait_send()

            return carry

        def drain_relay(w, carry):
            @pl.when(jnp.logical_not(is_me(relay_to(w))))
            def _():
                r_copy(c, w).wait_send()

            return carry

        lax.fori_loop(0, OWNERS, drain, 0)
        lax.fori_loop(0, 4, drain_relay, 0)
    for store in stores:
        store.wait()


def finish(*args):
    ins, outs, held, (weights, aweights, in_sem, out_sem) = args[0:5], args[5:11], args[11:16], args[16:20]
    out_tiles = held[4]
    loads = [pltpu.make_async_copy(ins[i], held[i], in_sem.at[i]) for i in range(5)]
    results = held[0:4] + (weights, aweights)
    stores = [pltpu.make_async_copy(results[i], outs[i], out_sem.at[i]) for i in range(6)]
    for i in (4, 0, 1, 2, 3):
        loads[i].start()
    loads[4].wait()
    for tile in range(TILES):
        matrix, column = tile_place(tile)
        width = tile_width(tile)
        columns = slice(LANES * column, LANES * column + width)
        if matrix < 3:
            weights[matrix, :, columns] = out_tiles[tile, :, 0:width]
        else:
            aweights[:, columns] = out_tiles[tile]
    stores[4].start()
    stores[5].start()
    for i in range(4):
        loads[i].wait()
        stores[i].start()
    for store in stores:
        store.wait()


def local(mlp_deltas, mlp_master, mlp_momentum, attn_deltas, attn_master, attn_momentum):
    x, ax = mlp_deltas[0], attn_deltas[0]
    mlp_master, mlp_momentum = (a.transpose(1, 0, 2) for a in (mlp_master, mlp_momentum))
    rows = x.shape[1]
    f32, bf16 = jnp.float32, jnp.bfloat16
    ins = (x, mlp_master, mlp_momentum, ax, attn_master, attn_momentum)
    owned = (mlp_master, mlp_momentum, attn_master, attn_momentum)
    scratch = [pltpu.VMEM(a.shape, a.dtype) for a in ins + owned]
    scratch += [
        pltpu.VMEM((TILES, rows, LANES), bf16),
        pltpu.VMEM((GROUPS, PART, rows, LANES), bf16),
        pltpu.VMEM((PART, rows, LANES), f32),
        pltpu.VMEM((TILES, rows, LANES), bf16),
    ]
    for _, n in CHUNKS:
        shape = (OWNERS, chunk_rows(n), LANES)
        for kind in (f32, bf16, bf16, f32, f32, bf16, bf16):
            scratch.append(pltpu.VMEM(shape, kind))
    count = len(CHUNKS)
    DMA = pltpu.SemaphoreType.DMA
    scratch += [
        DMA((count, GROUPS)), DMA((count, GROUPS)),
        DMA((count, OWNERS)), DMA((count, OWNERS)),
        DMA((count, OWNERS)), DMA((count, OWNERS)),
        DMA((count, 4)), DMA((count, 4)),
        DMA((count, GROUPS)), DMA((count, GROUPS)),
        DMA(()), DMA((6,)), DMA((4 + count,)),
    ]
    shapes = [jax.ShapeDtypeStruct(a.shape, a.dtype) for a in owned]
    landed = jax.ShapeDtypeStruct((TILES, rows, LANES), bf16)
    anywhere = pl.BlockSpec(memory_space=pl.ANY)
    results = pl.pallas_call(
        kernel,
        out_shape=shapes + [landed],
        in_specs=[anywhere] * 6,
        out_specs=[anywhere] * 5,
        scratch_shapes=scratch,
        compiler_params=pltpu.CompilerParams(collective_id=0, has_side_effects=True),
    )(*ins)
    blocks = [jax.ShapeDtypeStruct(a.shape, a.dtype) for a in (x, ax)]
    master, momentum, amaster, amomentum, weights, aweights = pl.pallas_call(
        finish,
        out_shape=shapes + blocks,
        in_specs=[anywhere] * 5,
        out_specs=[anywhere] * 6,
        scratch_shapes=[pltpu.VMEM(a.shape, a.dtype) for a in shapes + [landed] + blocks]
        + [DMA((5,)), DMA((6,))],
    )(*results)
    return (
        master.transpose(1, 0, 2), momentum.transpose(1, 0, 2), weights,
        amaster, amomentum, aweights,
    )


def solution(mesh):
    owned = P(None, ("group", "shard", "tensor"), None)
    attn_owned = P(("group", "shard", "tensor"), None)
    return jax.shard_map(
        local,
        mesh=mesh,
        in_specs=(
            P("group", None, "shard", "tensor"), owned, owned,
            P("group", "shard", "tensor"), attn_owned, attn_owned,
        ),
        out_specs=(
            owned, owned, P(None, "shard", "tensor"),
            attn_owned, attn_owned, P("shard", "tensor"),
        ),
        check_vma=False,
    )
```
